32 devices in a mesh: fsdp: 8 (over z, x), ctx: 2 (over y), tp: 2 (over core).
Axes of the slice: x: 2, y: 2, z: 4, core: 2. Of those that a mesh axis runs over, the one named last changes fastest.
Arguments:
- tokens: float32 [2048, 1024], P(('fsdp', 'ctx')), may hold values from -6 to 6
- lengths: int32 [8, 4], P('fsdp'), may hold values from 1 to 128, 256 in all within a row
- wqkv: bfloat16 [1024, 3, 1024], P('fsdp', None, 'tp'), may hold values from -4 to 4
- wo: bfloat16 [1024, 1024], P('tp', 'fsdp'), may hold values from -3 to 3
- wi: bfloat16 [1024, 2, 2624], P('fsdp', None, 'tp'), may hold values from -0.1875 to 0.1875
- wout: bfloat16 [2624, 1024], P('tp', 'fsdp'), may hold values from -0.125 to 0.125
- gain_one: bfloat16 [1024], P('fsdp'), may hold values from 0.5 to 1.5
- gain_two: bfloat16 [1024], P('fsdp'), may hold values from 0.5 to 1.5
- cotangent: float32 [2048, 1024], P(('fsdp', 'ctx')), may hold values from -6 to 6
Outputs:
- output: float32 [2048, 1024], P(('fsdp', 'ctx'))
- token_input_grad: float32 [2048, 1024], P(('fsdp', 'ctx'))
- d_wqkv: float32 [1024, 3, 1024], P('fsdp', None, 'tp')
- d_wo: float32 [1024, 1024], P('tp', 'fsdp')
- d_wi: float32 [1024, 2, 2624], P('fsdp', None, 'tp')
- d_wout: float32 [2624, 1024], P('tp', 'fsdp')
- d_gain_one: float32 [1024], P('fsdp')
- d_gain_two: float32 [1024], P('fsdp')
The draws below stay inside these ranges and needn't reach their ends.
Inputs may be any that keep to these rules, and one draw needn't show every extreme that they name: Each row of lengths holds the 4 sequence lengths of one group; they sum to 256, and the longest is exactly 128.
All inputs are finite; a program needn't handle non-finite values.
Results may differ from the reference program's by a relative error of at most 0.019.
The reference program's roundings to bfloat16 on the way count: a program that leaves them out, or rounds other values in their place, can miss the bound.
Values may be sent and summed in bfloat16 or wider, within the bound.
No kernel may reach another device: no remote copies, remote signals or barrier semaphores. Data moves between devices by JAX's collectives and lax.ppermute only.
A program may use at most 128 MiB of HBM per device.

```python
import math
import jax
import jax.numpy as jnp
import numpy as np
from jax import lax

D = 1024
H = 16
DH = 64
FF = 2624
TOK_DEV = 128
SEQS = 4
ROWS = 256
TOKENS = 2048
N_FSDP = 8
N_CTX = 2


def draw_wqkv(key, part):
    base_key = jax.random.fold_in(key, 11)
    base = jax.random.truncated_normal(base_key, -4.0, 4.0, (D, 3, H * DH), jnp.float32) * D ** (-0.5)
    return jnp.clip(base, -4.0, 4.0).astype(jnp.bfloat16)


def steps_of(key, extent, shards, least, high):
    loudness, own = 1.0, jax.random.fold_in(key, 6)
    for dim, parts in shards:
        heights = jnp.exp(jax.random.uniform(jax.random.fold_in(own, dim), (parts,), jnp.float32, least / len(shards), high / len(shards)))
        loudness = loudness * jnp.repeat(heights, extent[dim] // parts).reshape([-1 if axis == dim else 1 for axis in range(len(extent))])
    return loudness


def split_up(amount, total, bound, lean):
    loads = [(1 << 20) // math.isqrt(rank ** lean) + 1 for rank in range(2, amount + 1)]
    spare, given = total - bound - (amount - 1), [1] * (amount - 1)
    while spare > 0:
        movable = [i for i in range(amount - 1) if given[i] < bound]
        pool, left = sum([loads[i] for i in movable]), spare
        for i in movable:
            extra = min(bound - given[i], max(1, left * loads[i] // pool), spare)
            given[i] = given[i] + extra
            spare = spare - extra
    return np.array([bound] + given)


def ragged(stream_key, amount, total, reach, skew):
    if amount == 2:
        one = jax.random.randint(stream_key, (), max(1, total - reach), min(reach, total - 1) + 1)
        return jnp.stack([one, total - one])
    sizes = jnp.asarray(split_up(amount, total, reach, skew), jnp.int32)
    pairs = (amount - 1) // 2
    donor, receiver = sizes[1:1 + 2 * pairs:2], sizes[2:2 + 2 * pairs:2]
    margin = jnp.minimum(donor - 1, reach - receiver)
    moved = jax.random.randint(jax.random.fold_in(stream_key, 1), (pairs,), 0, 1 << 20) % (margin + 1)
    sizes = sizes.at[1:1 + 2 * pairs:2].set(donor - moved).at[2:2 + 2 * pairs:2].set(receiver + moved)
    return sizes[jax.random.permutation(jax.random.fold_in(stream_key, 2), amount)]


def noise(rng, extent, deviation, reach, pieces=(), kind=jnp.bfloat16):
    entries = jax.random.normal(rng, extent, jnp.float32) * deviation
    if len(pieces) > 0:
        entries = steps_of(rng, extent, pieces, -0.22, 0.18) * entries
    return jnp.clip(entries, min=-reach, max=reach).astype(kind)


def setup_inputs(seed: int = 0) -> dict:
    key_of = jax.random.split(jax.random.key(seed), 10)
    tokens = noise(key_of[0], (TOKENS, D), 1.0, 6.0, ((0, 16),), jnp.float32)
    lengths = jax.vmap(lambda own: ragged(own, SEQS, ROWS, ROWS // 2, 2))(jax.random.split(key_of[1], N_FSDP)).reshape((N_FSDP, SEQS)).astype(jnp.int32)
    wqkv = draw_wqkv(jax.random.fold_in(key_of[9], 71), 0)
    wo = noise(key_of[3], (H * DH, D), (max(H * DH // 256, 1)) ** -0.5, 3.0, ((0, 2), (1, 8)))
    wi = noise(key_of[4], (D, 2, FF), D ** -0.5, 0.1875, ((0, 8), (2, 2)))
    wout = noise(key_of[5], (FF, D), FF ** -0.5, 0.125, ((0, 2), (1, 8)))
    gain_one = jnp.clip(1.0 + 0.1 * jax.random.normal(key_of[6], (D,), jnp.float32), 0.5, 1.5).astype(jnp.bfloat16)
    gain_two = jnp.clip(1.0 + 0.1 * jax.random.normal(key_of[7], (D,), jnp.float32), 0.5, 1.5).astype(jnp.bfloat16)
    cotangent = noise(key_of[8], (TOKENS, D), 1.0, 6.0, ((0, 16),), jnp.float32)
    return dict(tokens=tokens, lengths=lengths, wqkv=wqkv, wo=wo, wi=wi, wout=wout, gain_one=gain_one, gain_two=gain_two, cotangent=cotangent)


eps = 1e-05
rope_base = 160000.0

def apply_layer_norm(value):
    center = value - lax.optimization_barrier(jnp.mean(value, axis=-1, keepdims=True))
    variance = lax.optimization_barrier(jnp.mean(center * center, axis=-1, keepdims=True))
    inverse_scale = lax.rsqrt(variance + eps)
    return (center * inverse_scale, inverse_scale)

def norm_backward_pass(upstream_grad, normalized_rows, inverse_scale):
    first_residual = lax.optimization_barrier(jnp.mean(upstream_grad, axis=-1, keepdims=True))
    second_residual = lax.optimization_barrier(jnp.mean(upstream_grad * normalized_rows, axis=-1, keepdims=True))
    return (upstream_grad - first_residual - normalized_rows * second_residual) * inverse_scale

def rotary(position, size):
    half = size // 2
    freq = jnp.power(jnp.float32(rope_base), -2.0 * jnp.arange(half, dtype=jnp.float32) / size)
    angle = position.astype(jnp.float32)[:, None] * freq[None, :]
    return (jnp.cos(angle)[:, None, :], jnp.sin(angle)[:, None, :])

def rotate(value, cosine, sine):
    half = value.shape[-1] // 2
    first_residual, second_residual = (value[..., :half], value[..., half:])
    return jnp.concatenate([first_residual * cosine - second_residual * sine, second_residual * cosine + first_residual * sine], axis=-1)

def rotate_back(upstream_grad, cosine, sine):
    half = upstream_grad.shape[-1] // 2
    first_residual, second_residual = (upstream_grad[..., :half], upstream_grad[..., half:])
    return jnp.concatenate([first_residual * cosine + second_residual * sine, second_residual * cosine - first_residual * sine], axis=-1)

def gelu_parts(value):
    cdf = 0.5 * (1.0 + lax.erf(value * 0.7071067811865476))
    density = jnp.exp(-0.5 * value * value) * 0.3989422804014327
    return (value * cdf, cdf + value * density)

def doc_layout(lens, count):
    ends = jnp.cumsum(lens).astype(jnp.int32)
    index = jnp.arange(count, dtype=jnp.int32)
    past = (index[:, None] >= ends[None, :]).astype(jnp.int32)
    return (lax.optimization_barrier(jnp.sum(past, axis=1)), index - lax.optimization_barrier(jnp.sum(past * lens[None, :], axis=1)))

def head_forward(query, keys, values, same, scale):
    score = jnp.dot(query, keys.T, preferred_element_type=jnp.float32) * scale
    score = jnp.where(same, score, -1e+30)
    top = lax.optimization_barrier(jnp.max(score, axis=1, keepdims=True))
    lse = top + jnp.log(lax.optimization_barrier(jnp.sum(jnp.exp(score - top), axis=1, keepdims=True)))
    prob = jnp.exp(score - lse).astype(jnp.bfloat16)
    return (jnp.dot(prob, values, preferred_element_type=jnp.float32).astype(jnp.bfloat16), lse[:, 0])

def head_backward(query, keys, values, same, lse, attn, dout, scale):
    score = jnp.dot(query, keys.T, preferred_element_type=jnp.float32) * scale
    score = jnp.where(same, score, -1e+30)
    prob = jnp.exp(score - lse[:, None])
    d_values = jnp.dot(prob.astype(jnp.bfloat16).T, dout, preferred_element_type=jnp.float32)
    d_prob = jnp.dot(dout, values.T, preferred_element_type=jnp.float32)
    delta = lax.optimization_barrier(jnp.sum(dout.astype(jnp.float32) * attn.astype(jnp.float32), axis=1, keepdims=True))
    d_score = (prob * (d_prob - delta) * scale).astype(jnp.bfloat16)
    d_query = jnp.dot(d_score, keys, preferred_element_type=jnp.float32)
    d_keys = jnp.dot(d_score.T, query, preferred_element_type=jnp.float32)
    return (d_query, d_keys, d_values)

def group_pass(norm_input_rows, norm_output_grad, lens, wqkv, wo, wi, wout, gain_one, gain_two):
    count = norm_input_rows.shape[0]
    seq, position = doc_layout(lens, count)
    same = seq[:, None] == seq[None, :]
    cosine, sine = rotary(position, DH)
    scale = DH ** (-0.5)
    first_norm_gain = gain_one.astype(jnp.float32)
    second_norm_gain = gain_two.astype(jnp.float32)
    w_qkv = wqkv.reshape(D, 3 * H * DH)
    w_in = wi.reshape(D, 2 * FF)
    normalized_rows1, inverse_scale1 = apply_layer_norm(norm_input_rows)
    first_norm_input = (normalized_rows1 * first_norm_gain).astype(jnp.bfloat16)
    qkv = jnp.dot(first_norm_input, w_qkv, preferred_element_type=jnp.float32).reshape(count, 3, H, DH)
    query = rotate(qkv[:, 0], cosine, sine).astype(jnp.bfloat16).transpose(1, 0, 2)
    keys = rotate(qkv[:, 1], cosine, sine).astype(jnp.bfloat16).transpose(1, 0, 2)
    values = qkv[:, 2].astype(jnp.bfloat16).transpose(1, 0, 2)
    attn_t, lse_t = lax.map(lambda item: head_forward(item[0], item[1], item[2], same, scale), (query, keys, values))
    attn = attn_t.transpose(1, 0, 2).reshape(count, H * DH)
    middle_state = norm_input_rows + jnp.dot(attn, wo, preferred_element_type=jnp.float32)
    normalized_rows2, inverse_scale2 = apply_layer_norm(middle_state)
    second_norm_input = (normalized_rows2 * second_norm_gain).astype(jnp.bfloat16)
    gated = jnp.dot(second_norm_input, w_in, preferred_element_type=jnp.float32).reshape(count, 2, FF)
    gate, upper = (gated[:, 0], gated[:, 1])
    active, slope = gelu_parts(gate)
    hidden = (active * upper).astype(jnp.bfloat16)
    output = middle_state + jnp.dot(hidden, wout, preferred_element_type=jnp.float32)
    dyb = norm_output_grad.astype(jnp.bfloat16)
    d_wout = jnp.dot(hidden.T, dyb, preferred_element_type=jnp.float32)
    d_hidden = jnp.dot(dyb, wout.T, preferred_element_type=jnp.float32)
    d_gated = jnp.stack([d_hidden * upper * slope, d_hidden * active], axis=1).astype(jnp.bfloat16).reshape(count, 2 * FF)
    d_wi = jnp.dot(second_norm_input.T, d_gated, preferred_element_type=jnp.float32).reshape(D, 2, FF)
    second_norm_input_grad = jnp.dot(d_gated, w_in.T, preferred_element_type=jnp.float32)
    second_gain_grad = lax.optimization_barrier(jnp.sum(second_norm_input_grad * normalized_rows2, axis=0))
    middle_state_grad = norm_output_grad + norm_backward_pass(second_norm_input_grad * second_norm_gain, normalized_rows2, inverse_scale2)
    d_midb = middle_state_grad.astype(jnp.bfloat16)
    d_wo = jnp.dot(attn.T, d_midb, preferred_element_type=jnp.float32)
    dout = jnp.dot(d_midb, wo.T, preferred_element_type=jnp.float32).astype(jnp.bfloat16)
    dout = dout.reshape(count, H, DH).transpose(1, 0, 2)
    dq_t, dk_t, dv_t = lax.map(lambda item: head_backward(item[0], item[1], item[2], same, item[3], item[4], item[5], scale), (query, keys, values, lse_t, attn_t, dout))
    d_query = rotate_back(dq_t.transpose(1, 0, 2), cosine, sine)
    d_keys = rotate_back(dk_t.transpose(1, 0, 2), cosine, sine)
    d_values = dv_t.transpose(1, 0, 2)
    d_qkv = jnp.stack([d_query, d_keys, d_values], axis=1).astype(jnp.bfloat16).reshape(count, 3 * H * DH)
    d_wqkv = jnp.dot(first_norm_input.T, d_qkv, preferred_element_type=jnp.float32).reshape(D, 3, H * DH)
    first_norm_input_grad = jnp.dot(d_qkv, w_qkv.T, preferred_element_type=jnp.float32)
    first_gain_grad = lax.optimization_barrier(jnp.sum(first_norm_input_grad * normalized_rows1, axis=0))
    norm_input_grad = middle_state_grad + norm_backward_pass(first_norm_input_grad * first_norm_gain, normalized_rows1, inverse_scale1)
    return (output, norm_input_grad, (d_wqkv, d_wo, d_wi, d_wout, first_gain_grad, second_gain_grad))

def reference(tokens, lengths, wqkv, wo, wi, wout, gain_one, gain_two, cotangent):
    count = TOK_DEV * N_CTX
    xs = tokens.reshape(N_FSDP, count, D)
    dys = cotangent.reshape(N_FSDP, count, D)
    start = (jnp.zeros((D, 3, H * DH), jnp.float32), jnp.zeros((H * DH, D), jnp.float32), jnp.zeros((D, 2, FF), jnp.float32), jnp.zeros((FF, D), jnp.float32), jnp.zeros((D,), jnp.float32), jnp.zeros((D,), jnp.float32))

    def step(carry, item):
        output, norm_input_grad, grads = group_pass(item[0], item[1], item[2], wqkv, wo, wi, wout, gain_one, gain_two)
        return (jax.tree.map(lambda a, b: a + b, carry, grads), (output, norm_input_grad))
    grads, (outs, d_xs) = lax.scan(step, start, (xs, dys, lengths))
    return (outs.reshape(TOKENS, D), d_xs.reshape(TOKENS, D), grads[0], grads[1], grads[2], grads[3], grads[4], grads[5])
```

```python
import functools

import jax
import jax.numpy as jnp
from jax import lax
from jax.experimental import pallas as pl
from jax.experimental.pallas import tpu as pltpu
from jax.sharding import PartitionSpec as P

DH = 64
eps = 1e-05
rope_base = 160000.0
f32 = jnp.float32
bf16 = jnp.bfloat16


NT = (((1,), (1,)), ((), ()))
NN = (((1,), (0,)), ((), ()))


def dot_nt(a, b):
    return lax.dot_general(a, b, NT, preferred_element_type=f32)


def dot_nn(a, b):
    return lax.dot_general(a, b, NN, preferred_element_type=f32)


VMEM = pl.BlockSpec(memory_space=pltpu.VMEM)
SMEM = pl.BlockSpec(memory_space=pltpu.SMEM)


def call(kernel, name, args, outs, scratch=(), flops=0):
    specs = [SMEM if a.dtype == jnp.int32 else VMEM for a in args]
    moved = sum(a.size * a.dtype.itemsize for a in args) + sum(
        o.size * o.dtype.itemsize for o in outs
    )
    return pl.pallas_call(
        kernel,
        out_shape=outs,
        in_specs=specs,
        out_specs=[VMEM] * len(outs),
        scratch_shapes=list(scratch),
        name=name,
        compiler_params=pltpu.CompilerParams(vmem_limit_bytes=60 * 1024 * 1024),
        cost_estimate=pl.CostEstimate(flops=int(flops), bytes_accessed=int(moved), transcendentals=0),
    )(*args)


def sds(shape, dtype):
    return jax.ShapeDtypeStruct(shape, dtype)


def normalize(u):
    center = u - jnp.mean(u, axis=-1, keepdims=True)
    inverse_scale = lax.rsqrt(jnp.mean(center * center, axis=-1, keepdims=True) + eps)
    return center * inverse_scale, inverse_scale


def norm_back(t, xhat, inverse_scale):
    first = jnp.mean(t, axis=-1, keepdims=True)
    second = jnp.mean(t * xhat, axis=-1, keepdims=True)
    return (t - first - xhat * second) * inverse_scale


def swap_halves(x):
    width = x.shape[1]
    half = DH // 2
    if width % 128:
        parts = []
        for h in range(width // DH):
            parts += [x[:, h * DH + half : (h + 1) * DH], x[:, h * DH : h * DH + half]]
        return jnp.concatenate(parts, axis=1)
    lane = lax.broadcasted_iota(jnp.int32, x.shape, 1)
    up = pltpu.roll(x, width - half, 1)
    down = pltpu.roll(x, half, 1)
    return jnp.where(lane % DH < half, up, down)


def sequence_mask(lens_ref, rows):
    row = lax.broadcasted_iota(jnp.int32, (rows, 1), 0)
    col = lax.broadcasted_iota(jnp.int32, (1, rows), 1)
    seq_row = jnp.zeros((rows, 1), jnp.int32)
    seq_col = jnp.zeros((1, rows), jnp.int32)
    end = jnp.int32(0)
    for s in range(lens_ref.shape[0]):
        end = end + lens_ref[s]
        seq_row = seq_row + (row >= end).astype(jnp.int32)
        seq_col = seq_col + (col >= end).astype(jnp.int32)
    return seq_row == seq_col


def blocks(pieces, index):
    width = pieces[0].shape[1]
    return [pl.ds(pl.multiple_of((index ^ k) * width, 128), width) for k in range(len(pieces))]


def split_halves(acc_ref, t, keep_ref, send_ref):
    half = acc_ref.shape[1] // 2
    keep_ref[...] = acc_ref[:, pl.ds(pl.multiple_of(t * half, 128), half)].astype(keep_ref.dtype)
    send_ref[...] = acc_ref[:, pl.ds(pl.multiple_of((1 - t) * half, 128), half)].astype(
        send_ref.dtype
    )


def join_halves(t, mine_ref, other_ref, full_ref):
    half = mine_ref.shape[1]
    full_ref[:, pl.ds(pl.multiple_of(t * half, 128), half)] = mine_ref[...].astype(full_ref.dtype)
    full_ref[:, pl.ds(pl.multiple_of((1 - t) * half, 128), half)] = other_ref[...].astype(
        full_ref.dtype
    )


def owned_rows(rows, own, c):
    row = lax.broadcasted_iota(jnp.int32, (rows, 1), 0)
    return (row >= c * own) & (row < (c + 1) * own)


def attention_forward_kernel(n, heads, own, where_ref, lens_ref, tok_ref, cos_ref, sin_ref, *refs):
    pieces = refs[:n]
    keep_ref, send_ref, a1_ref, q_ref, k_ref, v_ref, attn_ref, lse_ref, gains_ref, acc_ref = refs[n:]
    index, c, t = where_ref[0], where_ref[1], where_ref[2]
    rows, width = tok_ref.shape
    cols = heads * DH
    cut = blocks(pieces, index)
    for k in range(n):
        gains_ref[:, cut[k]] = pieces[k][4 * cols : 4 * cols + 16, :].astype(f32)
    xhat, _ = normalize(tok_ref[...])
    a1_ref[...] = (xhat * gains_ref[0:1, :]).astype(bf16)
    qkv = [jnp.zeros((rows, cols), f32) for _ in range(3)]
    for k in range(n):
        left = a1_ref[:, cut[k]]
        for j in range(3):
            qkv[j] = qkv[j] + dot_nt(left, pieces[k][j * cols : (j + 1) * cols, :])
    cosine, sine = cos_ref[...], sin_ref[...]
    q_ref[...] = (qkv[0] * cosine + swap_halves(qkv[0]) * sine).astype(bf16)
    k_ref[...] = (qkv[1] * cosine + swap_halves(qkv[1]) * sine).astype(bf16)
    v_ref[...] = qkv[2].astype(bf16)
    same = sequence_mask(lens_ref, rows)
    scale = DH ** (-0.5)
    for h in range(heads):
        head = slice(h * DH, (h + 1) * DH)
        score = dot_nt(q_ref[:, head], k_ref[:, head]) * scale
        score = jnp.where(same, score, -1e30)
        top = jnp.max(score, axis=1, keepdims=True)
        lse = top + jnp.log(jnp.sum(jnp.exp(score - top), axis=1, keepdims=True))
        prob = jnp.exp(score - lse).astype(bf16)
        attn_ref[:, head] = dot_nn(prob, v_ref[:, head]).astype(bf16)
        lse_ref[:, h : h + 1] = lse
    attn = attn_ref[...]
    for k in range(n):
        acc_ref[:, cut[k]] = dot_nn(attn, pieces[k][3 * cols : 4 * cols, :])
    half = width // 2
    mine = pl.ds(pl.multiple_of(t * half, 128), half)
    owned = owned_rows(rows, own, c)
    keep_ref[...] = acc_ref[:, mine] + jnp.where(owned, tok_ref[:, mine], 0.0)
    send_ref[...] = acc_ref[:, pl.ds(pl.multiple_of((1 - t) * half, 128), half)]


def mlp_kernel(n, where_ref, mine_ref, other_ref, gain_ref, dyb_ref, *refs):
    pieces = refs[:n]
    (
        out_keep_ref, out_send_ref, da_keep_ref, da_send_ref,
        a2_ref, hid_ref, dgate_ref, dup_ref, mid_ref, acc_ref,
    ) = refs[n:]
    index, t = where_ref[0], where_ref[2]
    rows = mine_ref.shape[0]
    hidden = hid_ref.shape[1]
    cut = blocks(pieces, index)
    join_halves(t, mine_ref, other_ref, mid_ref)
    xhat, _ = normalize(mid_ref[...])
    a2_ref[...] = (xhat * gain_ref[1:2, :]).astype(bf16)
    gate = jnp.zeros((rows, hidden), f32)
    up = jnp.zeros((rows, hidden), f32)
    dhid = jnp.zeros((rows, hidden), f32)
    for k in range(n):
        left = a2_ref[:, cut[k]]
        gate = gate + dot_nt(left, pieces[k][0:hidden, :])
        up = up + dot_nt(left, pieces[k][hidden : 2 * hidden, :])
        dhid = dhid + dot_nt(dyb_ref[:, cut[k]], pieces[k][2 * hidden : 3 * hidden, :])
    cdf = 0.5 * (1.0 + lax.erf(gate * 0.7071067811865476))
    density = jnp.exp(-0.5 * gate * gate) * 0.3989422804014327
    active = gate * cdf
    slope = cdf + gate * density
    hid_ref[...] = (active * up).astype(bf16)
    dgate_ref[...] = (dhid * up * slope).astype(bf16)
    dup_ref[...] = (dhid * active).astype(bf16)
    dgate, dup = dgate_ref[...], dup_ref[...]
    for k in range(n):
        acc_ref[:, cut[k]] = dot_nn(dgate, pieces[k][0:hidden, :]) + dot_nn(
            dup, pieces[k][hidden : 2 * hidden, :]
        )
    split_halves(acc_ref, t, da_keep_ref, da_send_ref)
    hid = hid_ref[...]
    for k in range(n):
        acc_ref[:, cut[k]] = dot_nn(hid, pieces[k][2 * hidden : 3 * hidden, :])
    split_halves(acc_ref, t, out_keep_ref, out_send_ref)


def weight_grad_kernel(n, lefts, where_ref, *refs):
    index = where_ref[0]
    ins, outs = refs[: 2 * lefts], refs[2 * lefts :]
    cut = blocks(outs, index)
    at = 0
    for p in range(lefts):
        left, right = ins[2 * p], ins[2 * p + 1]
        turned = left[...].T
        for k in range(n):
            outs[k][at : at + left.shape[1], :] = dot_nn(turned, right[:, cut[k]]).astype(
                outs[k].dtype
            )
        at += left.shape[1]


def attention_backward_kernel(
    n, heads, own, where_ref, lens_ref, da_mine_ref, da_other_ref, mid_mine_ref, mid_other_ref,
    gain_ref, dyb_ref, cot_ref, cos_ref, sin_ref, q_ref, k_ref, v_ref, attn_ref, lse_ref, *refs
):
    pieces = refs[:n]
    (
        dmid_ref, dmidb_ref, dq_ref, dk_ref, dv_ref, dgain_ref, keep_ref, send_ref,
        full_ref, xhat_ref,
    ) = refs[n:]
    index, c, t = where_ref[0], where_ref[1], where_ref[2]
    cols = heads * DH
    cut = blocks(pieces, index)
    join_halves(t, mid_mine_ref, mid_other_ref, full_ref)
    xhat, inverse_scale = normalize(full_ref[...])
    xhat_ref[...] = xhat
    join_halves(t, da_mine_ref, da_other_ref, full_ref)
    rows = full_ref.shape[0]
    start = pl.multiple_of(c * own, 8)
    dgain_ref[...] = jnp.broadcast_to(
        jnp.sum(
            full_ref[pl.ds(start, own), :] * xhat_ref[pl.ds(start, own), :], axis=0, keepdims=True
        ),
        dgain_ref.shape,
    )
    back = norm_back(full_ref[...] * gain_ref[1:2, :], xhat, inverse_scale)
    full_ref[...] = back
    dmid_own = cot_ref[...] + full_ref[pl.ds(start, own), :]
    dmid_ref[...] = dmid_own
    dmidb_ref[...] = (dyb_ref[...].astype(f32) + back).astype(bf16)
    dmidb_ref[pl.ds(pl.multiple_of(c * own, 16), own), :] = dmid_own.astype(bf16)
    dout = jnp.zeros((rows, cols), f32)
    for k in range(n):
        dout = dout + dot_nt(dmidb_ref[:, cut[k]], pieces[k][3 * cols : 4 * cols, :])
    doutb = dout.astype(bf16)
    cosine, sine = cos_ref[...], sin_ref[...]
    same = sequence_mask(lens_ref, rows)
    scale = DH ** (-0.5)
    dqs, dks = [], []
    for h in range(heads):
        head = slice(h * DH, (h + 1) * DH)
        q, key, value = q_ref[:, head], k_ref[:, head], v_ref[:, head]
        dh = doutb[:, head]
        score = dot_nt(q, key) * scale
        score = jnp.where(same, score, -1e30)
        prob = jnp.exp(score - lse_ref[:, h : h + 1])
        dv_ref[:, head] = dot_nn(prob.astype(bf16).T, dh).astype(bf16)
        dprob = dot_nt(dh, value)
        delta = jnp.sum(
            dh.astype(f32) * attn_ref[:, head].astype(f32), axis=1, keepdims=True
        )
        ds = (prob * (dprob - delta) * scale).astype(bf16)
        dqs.append(dot_nn(ds, key))
        dks.append(dot_nn(ds.T, q))
    dq = jnp.concatenate(dqs, axis=1) if heads > 1 else dqs[0]
    dk = jnp.concatenate(dks, axis=1) if heads > 1 else dks[0]
    dq_ref[...] = (dq * cosine - swap_halves(dq) * sine).astype(bf16)
    dk_ref[...] = (dk * cosine - swap_halves(dk) * sine).astype(bf16)
    dq, dk, dv = dq_ref[...], dk_ref[...], dv_ref[...]
    for k in range(n):
        full_ref[:, cut[k]] = (
            dot_nn(dq, pieces[k][0:cols, :])
            + dot_nn(dk, pieces[k][cols : 2 * cols, :])
            + dot_nn(dv, pieces[k][2 * cols : 3 * cols, :])
        )
    split_halves(full_ref, t, keep_ref, send_ref)


def input_grad_kernel(
    where_ref, mine_ref, other_ref, tok_ref, gain_ref, dmid_ref, grad_ref, dgain_ref, full_ref
):
    join_halves(where_ref[2], mine_ref, other_ref, full_ref)
    xhat, inverse_scale = normalize(tok_ref[...])
    da = full_ref[...]
    dgain_ref[...] = jnp.broadcast_to(jnp.sum(da * xhat, axis=0, keepdims=True), dgain_ref.shape)
    grad_ref[...] = dmid_ref[...] + norm_back(da * gain_ref[0:1, :], xhat, inverse_scale)


def rounded(x, multiple):
    return -(-x // multiple) * multiple


def body(tokens, lengths, wqkv, wo, wi, wout, gain_one, gain_two, cotangent):
    n = lax.axis_size("fsdp")
    nc = lax.axis_size("ctx")
    own, width = tokens.shape
    rows = own * nc
    half = width // 2
    index, c, t = lax.axis_index("fsdp"), lax.axis_index("ctx"), lax.axis_index("tp")
    where = jnp.stack([index, c, t]).astype(jnp.int32)
    lens = lengths[0]
    block = width // n
    by_pieces = n & (n - 1) == 0 and block % 128 == 0
    count = n if by_pieces else 1

    def xor(x, k):
        return lax.ppermute(x, "fsdp", [(a, a ^ k) for a in range(n)])

    def over_cores(x):
        return lax.ppermute(x, "tp", [(0, 1), (1, 0)])

    def over_ctx(x):
        return lax.ppermute(x, "ctx", [(0, 1), (1, 0)])

    def all_rows(x):
        if nc != 2:
            return lax.all_gather(x, "ctx", axis=0, tiled=True)
        other = over_ctx(x)
        return jnp.where(
            c == 0, jnp.concatenate([x, other], axis=0), jnp.concatenate([other, x], axis=0)
        )

    def gather(piece):
        if not by_pieces:
            return [lax.all_gather(piece, "fsdp", axis=1, tiled=True)]
        pieces = [None] * n
        pieces[0] = piece
        for k in range(2, n, 2):
            pieces[k] = xor(piece, k)
        for k in range(0, n, 2):
            pieces[k + 1] = xor(pieces[k], 1)
        return pieces

    def reduce_pieces(pieces):
        if not by_pieces:
            return lax.psum_scatter(
                pieces[0].astype(f32), "fsdp", scatter_dimension=1, tiled=True
            )
        total = None
        for k in list(range(2, n, 2)) + [0]:
            pair = pieces[k].astype(f32) + xor(pieces[k + 1], 1).astype(f32)
            if k:
                pair = xor(pair.astype(bf16), k).astype(f32)
            total = pair if total is None else total + pair
        return total

    def sum_everywhere(keep, send):
        part = keep + over_cores(send)
        if nc == 2:
            full = part + over_ctx(part.astype(bf16)).astype(f32)
        else:
            full = lax.psum(part, "ctx")
        return full, over_cores(full)

    def sum_to_owner(keep, send):
        part = keep.astype(f32) + over_cores(send).astype(f32)
        if nc == 2:
            first, second = part[:own], part[own:]
            theirs = jnp.where(c == 0, second, first).astype(bf16)
            full = jnp.where(c == 0, first, second) + over_ctx(theirs).astype(f32)
        else:
            full = lax.psum_scatter(part, "ctx", scatter_dimension=0, tiled=True)
        return full, over_cores(full)

    cols_tp = wqkv.shape[2]
    hid_tp = wi.shape[2]
    cols = cols_tp // nc
    hidden = hid_tp // nc
    pad = rounded(hidden, 16) - hidden
    heads = cols // DH

    def quarter(x, size, axis):
        return lax.dynamic_slice_in_dim(x, c * size, size, axis)

    qkv_own = quarter(wqkv, cols, 2).transpose(1, 2, 0).reshape(3 * cols, block)
    gains_own = jnp.concatenate(
        [gain_one[None], gain_two[None], jnp.zeros((14, block), bf16)], axis=0
    )
    attn_own = jnp.concatenate([qkv_own, quarter(wo, cols, 0), gains_own], axis=0)
    wi_own = quarter(wi, hidden, 2).transpose(1, 2, 0)
    wout_own = quarter(wout, hidden, 0)
    if pad:
        wi_own = jnp.pad(wi_own, ((0, 0), (0, pad), (0, 0)))
        wout_own = jnp.pad(wout_own, ((0, pad), (0, 0)))
    hid_pad = hidden + pad
    mlp_own = jnp.concatenate([wi_own.reshape(2 * hid_pad, block), wout_own], axis=0)

    attn_pieces = gather(attn_own)
    tok_all = all_rows(tokens)
    mlp_pieces = gather(mlp_own)
    dyb_all = all_rows(cotangent.astype(bf16))

    ends = [jnp.int32(0)]
    for s in range(lens.shape[0]):
        ends.append(ends[-1] + lens[s])
    row = jnp.arange(rows, dtype=jnp.int32)
    position = row
    for s in range(lens.shape[0]):
        position = position - jnp.where(row >= ends[s + 1], lens[s], 0)
    freq = jnp.power(f32(rope_base), -2.0 * jnp.arange(DH // 2, dtype=f32) / DH)
    angle = position.astype(f32)[:, None] * freq[None, :]
    cosine, sine = jnp.cos(angle), jnp.sin(angle)
    cosine = jnp.tile(cosine, (1, 2 * heads))
    sine = jnp.tile(jnp.concatenate([-sine, sine], axis=1), (1, heads))

    wide = sds((rows, cols), bf16)
    keep, send, a1, query, keys, values, attn, lse, gains = call(
        functools.partial(attention_forward_kernel, count, heads, own),
        "attention_forward",
        [where, lens, tok_all, cosine, sine] + attn_pieces,
        [
            sds((rows, half), f32), sds((rows, half), f32), sds((rows, width), bf16),
            wide, wide, wide, wide, sds((rows, heads), f32), sds((16, width), f32),
        ],
        [pltpu.VMEM((rows, width), f32)],
        flops=8 * rows * width * cols + 4 * rows * rows * cols,
    )
    mid_mine, mid_other = sum_everywhere(keep, send)

    deep = sds((rows, hid_pad), bf16)
    out_keep, out_send, da_keep, da_send, a2, hid, dgate, dup = call(
        functools.partial(mlp_kernel, count),
        "mlp",
        [where, mid_mine, mid_other, gains, dyb_all] + mlp_pieces,
        [
            sds((rows, half), f32), sds((rows, half), bf16), sds((rows, half), f32),
            sds((rows, half), f32), sds((rows, width), bf16), deep, deep, deep,
        ],
        [pltpu.VMEM((rows, width), f32), pltpu.VMEM((rows, width), f32)],
        flops=14 * rows * width * hid_pad,
    )
    da2_mine, da2_other = sum_everywhere(da_keep, da_send)
    mlp_grads = call(
        functools.partial(weight_grad_kernel, count, 3),
        "mlp_weight_grads",
        [where, dgate, a2, dup, a2, hid, dyb_all],
        [sds((3 * hid_pad, width // count), bf16 if by_pieces else f32)] * count,
        flops=6 * rows * width * hid_pad,
    )
    mlp_owned = reduce_pieces(mlp_grads)
    out_mine, out_other = sum_to_owner(out_keep, out_send)

    dmid, dmidb, dq, dk, dv, dgain_two, da_keep, da_send = call(
        functools.partial(attention_backward_kernel, count, heads, own),
        "attention_backward",
        [
            where, lens, da2_mine, da2_other, mid_mine, mid_other, gains, dyb_all, cotangent,
            cosine, sine, query, keys, values, attn, lse,
        ]
        + attn_pieces,
        [
            sds((own, width), f32), sds((rows, width), bf16), wide, wide, wide,
            sds((8, width), f32), sds((rows, half), f32), sds((rows, half), f32),
        ],
        [pltpu.VMEM((rows, width), f32), pltpu.VMEM((rows, width), f32)],
        flops=8 * rows * width * cols + 10 * rows * rows * cols,
    )
    attn_grads = call(
        functools.partial(weight_grad_kernel, count, 4),
        "attention_weight_grads",
        [where, dq, a1, dk, a1, dv, a1, attn, dmidb],
        [sds((4 * cols, width // count), bf16 if by_pieces else f32)] * count,
        flops=8 * rows * width * cols,
    )
    attn_owned = reduce_pieces(attn_grads)
    da1_mine, da1_other = sum_to_owner(da_keep, da_send)
    token_grad, dgain_one = call(
        input_grad_kernel,
        "input_grad",
        [where, da1_mine, da1_other, tokens, gains, dmid],
        [sds((own, width), f32), sds((8, width), f32)],
        [pltpu.VMEM((own, width), f32)],
    )

    dgains = jnp.concatenate([dgain_one[:1], dgain_two[:1]], axis=0)
    if by_pieces:
        spread = dgains.reshape(2, n, block)
        total = spread
        for bit in range(n.bit_length() - 1):
            total = total + xor(total, 1 << bit)
        if nc == 2:
            total = total + over_ctx(total)
        else:
            total = lax.psum(total, "ctx")
        owned_gains = lax.dynamic_index_in_dim(total, index, 1, keepdims=False)
    else:
        owned_gains = lax.psum(
            lax.psum_scatter(dgains, "fsdp", scatter_dimension=1, tiled=True), "ctx"
        )

    def all_quarters(x):
        if nc != 2:
            return lax.all_gather(x, "ctx", axis=0)
        other = over_ctx(x.astype(bf16)).astype(f32)
        return jnp.where(c == 0, jnp.stack([x, other]), jnp.stack([other, x]))

    attn_full = all_quarters(attn_owned)
    mlp_full = all_quarters(mlp_owned)
    d_wqkv = (
        attn_full[:, : 3 * cols].reshape(nc, 3, cols, block).transpose(3, 1, 0, 2)
    ).reshape(block, 3, cols_tp)
    d_wo = attn_full[:, 3 * cols :].reshape(cols_tp, block)
    d_wi = mlp_full[:, : 2 * hid_pad].reshape(nc, 2, hid_pad, block)[:, :, :hidden]
    d_wi = d_wi.transpose(3, 1, 0, 2).reshape(block, 2, hid_tp)
    d_wout = mlp_full[:, 2 * hid_pad : 2 * hid_pad + hidden].reshape(hid_tp, block)

    left = jnp.where(t == 0, out_mine, out_other)
    right = jnp.where(t == 0, out_other, out_mine)
    mid_m = lax.dynamic_slice_in_dim(mid_mine, c * own, own, 0)
    mid_o = lax.dynamic_slice_in_dim(mid_other, c * own, own, 0)
    output = jnp.concatenate(
        [left + jnp.where(t == 0, mid_m, mid_o), right + jnp.where(t == 0, mid_o, mid_m)], axis=1
    )
    return (output, token_grad, d_wqkv, d_wo, d_wi, d_wout, owned_gains[0], owned_gains[1])


def solution(mesh):
    return jax.shard_map(
        body,
        mesh=mesh,
        in_specs=(
            P(("fsdp", "ctx"), None),
            P("fsdp", None),
            P("fsdp", None, "tp"),
            P("tp", "fsdp"),
            P("fsdp", None, "tp"),
            P("tp", "fsdp"),
            P("fsdp"),
            P("fsdp"),
            P(("fsdp", "ctx"), None),
        ),
        out_specs=(
            P(("fsdp", "ctx"), None),
            P(("fsdp", "ctx"), None),
            P("fsdp", None, "tp"),
            P("tp", "fsdp"),
            P("fsdp", None, "tp"),
            P("tp", "fsdp"),
            P("fsdp"),
            P("fsdp"),
        ),
        check_vma=False,
    )
```
